32 devices in a mesh: wide: 8 (over y, x, core), narrow: 4 (over z).
Axes of the slice: x: 2, y: 2, z: 4, core: 2. Of those that a mesh axis runs over, the one named last changes fastest.
Arguments:
- loads: bfloat16 [256, 262144], P('narrow', 'wide'), may hold values from -6 to 6
- state: bfloat16 [256, 262144], P('narrow', 'wide'), may hold values from -6 to 6
- modal_diag: float32 [262144], P('wide'), may hold values from 0.5 to 2
- phi: bfloat16 [2048, 128, 128], P('wide'), may hold values from -0.25 to 0.25
- incidence: int32 [2048], P('wide'), may hold values from 0 to 127
- sizes: int32 [1024], P('wide'), may hold values from 1 to 129, as said below
- factor: float32 [16384, 16384], P('wide', 'narrow'), may hold values from -0.046875 to 0.046875
Outputs:
- adjoint: bfloat16 [256, 262144], P('narrow', 'wide')
- sensitivity: float32 [256, 1024], P('narrow', 'wide')
The draws below stay inside these ranges and needn't reach their ends.
Inputs may be any that keep to these rules, and one draw needn't show every extreme that they name: `sizes`: the 128 substructures of each group hold at most 256 tiles together, and in every draw some group holds exactly 256.
All inputs are finite; a program needn't handle non-finite values.
Results may differ from the reference program's by a relative error of at most 0.015.
Values may be sent and summed in bfloat16 or wider, within the bound.
A program may use at most 128 MiB of HBM per device.

```python
import math
import jax
import jax.numpy as jnp
from jax import lax

MODES = 16384
BLOCK = 128
LOADS = 256
SUBS_DEV = 128
TILES_DEV = 256
SUBS = 1024
TILES = 2048
ROWS = 262144
MBLOCKS = 128


def draw_sizes(key, part):
    groups = SUBS // SUBS_DEV
    spare = TILES_DEV - SUBS_DEV
    first_key, second_key, third_key, fourth_key = jax.random.split(jax.random.fold_in(key, 7), 4)
    extra = jax.random.randint(first_key, (groups,), 0, spare + 1)
    fullest = jax.random.randint(second_key, (), 0, groups)
    heaviest = jax.random.randint(fourth_key, (), 0, SUBS_DEV)
    is_full = jnp.arange(groups) == fullest
    extra = jnp.where(is_full, spare, extra)
    targets = jax.random.randint(third_key, (groups, spare), 0, SUBS_DEV)
    targets = jnp.where(is_full[:, None], heaviest, targets)
    used = jnp.arange(spare)[None, :] < extra[:, None]
    hits = (targets[:, :, None] == jnp.arange(SUBS_DEV)[None, None, :]) & used[:, :, None]
    counts = jnp.sum(hits.astype(jnp.int32), axis=1)
    return (1 + counts).reshape(groups * SUBS_DEV).astype(jnp.int32)


def with_ends(result, own_key, low, top_value):
    longest = result.shape.index(max(result.shape))
    spots = []
    for shift in (0, 1):
        where = [jax.random.randint(jax.random.fold_in(own_key, axis), (), 0, length) for axis, length in enumerate(result.shape)]
        where[longest] = (where[longest] + shift) % result.shape[longest]
        spots.append(tuple(where))
    return result.at[spots[0]].set(low).at[spots[1]].set(top_value)


def steps_of(key, dims, shards, smallest, top_value):
    level = 1.0
    for position, shards_of in shards:
        steps = jax.random.uniform(jax.random.fold_in(jax.random.fold_in(key, 6), position), (shards_of,), jnp.float32, smallest / len(shards), top_value / len(shards))
        level = level * jnp.repeat(jnp.exp(steps), dims[position] // shards_of).reshape((-1,) + (1,) * (len(dims) - 1 - position))
    return level


def bell_draw(own_key, extent, spread, most, pieces=(), kind=jnp.bfloat16):
    factor_of = steps_of(own_key, extent, pieces, -0.22, 0.18) if pieces else 1.0
    drawn = jax.random.normal(own_key, extent, jnp.float32) * spread * factor_of
    return jnp.minimum(jnp.maximum(drawn, -most), most).astype(kind)


def setup_inputs(seed: int = 0) -> dict:
    keys = jax.random.split(jax.random.key(seed), 8)
    return {
        "loads": bell_draw(keys[0], (LOADS, ROWS), 1.0, 6.0, ((0, 4), (1, 8))),
        "state": bell_draw(keys[1], (LOADS, ROWS), 1.0, 6.0, ((0, 4), (1, 8))),
        "modal_diag": jnp.clip(jnp.exp(math.log(2.0) - 1.3862944 * jax.random.uniform(keys[2], (ROWS,), jnp.float32) ** steps_of(keys[2], (ROWS,), ((0, 8),), -0.2, 0.2)), 0.5, 2.0),
        "phi": bell_draw(keys[3], (TILES, BLOCK, BLOCK), (4 * BLOCK) ** -0.5, 0.25, ((0, 8),)),
        "incidence": with_ends(jax.random.randint(keys[4], (TILES,), 0, MBLOCKS), jax.random.fold_in(keys[4], 1), 0, MBLOCKS - 1).astype(jnp.int32),
        "sizes": draw_sizes(jax.random.fold_in(keys[7], 71), 0),
        "factor": bell_draw(keys[6], (MODES, MODES), MODES ** -0.5, 0.046875, ((0, 8), (1, 4)), jnp.float32),
    }


sens_scale = 0.0625


def reference(loads, state, modal_diag, phi, incidence, sizes, factor):
    groups = SUBS // SUBS_DEV
    block_count = MODES // BLOCK
    load_tiles = loads.reshape(LOADS, groups, TILES_DEV, BLOCK).transpose(1, 0, 2, 3)
    state_tiles = state.reshape(LOADS, groups, TILES_DEV, BLOCK).transpose(1, 0, 2, 3)
    diag_tiles = modal_diag.reshape(groups, TILES_DEV, BLOCK)
    phi_tiles = phi.reshape(groups, TILES_DEV, BLOCK, BLOCK)
    block_ids = incidence.reshape(groups, TILES_DEV)
    group_sizes = sizes.reshape(groups, SUBS_DEV)
    slot_index = jnp.arange(TILES_DEV, dtype=jnp.int32)

    def layout(group_size):
        running = jnp.cumsum(group_size)
        owner_sub = jnp.sum((running[None, :] <= slot_index[:, None]).astype(jnp.int32), axis=1)
        live_slot = slot_index < running[-1]
        return owner_sub, live_slot

    def condense(carry, item):
        load_part, phi_part, id_part, size_part = item
        owner_sub, live_slot = layout(size_part)
        tile_terms = jnp.einsum("lti,tim->tlm", load_part.astype(jnp.float32), phi_part.astype(jnp.float32))
        tile_terms = jnp.where(live_slot[:, None, None], tile_terms, jnp.zeros_like(tile_terms))
        summed = jax.ops.segment_sum(tile_terms, id_part, num_segments=block_count)
        return carry + summed, None

    start_sum = jnp.zeros((block_count, LOADS, BLOCK), jnp.float32)
    blocks_sum, _ = lax.scan(condense, start_sum, (load_tiles, phi_tiles, block_ids, group_sizes))
    condensed = blocks_sum.transpose(1, 0, 2).reshape(LOADS, MODES)
    image = jnp.dot(condensed, factor, precision=lax.Precision.HIGHEST)
    amplitude = jnp.dot(image, factor.T, precision=lax.Precision.HIGHEST)
    amp_round = amplitude.astype(jnp.bfloat16).reshape(LOADS, block_count, BLOCK)

    def recover(item):
        load_part, state_part, diag_part, phi_part, id_part, size_part = item
        owner_sub, live_slot = layout(size_part)
        picked = jnp.take(amp_round, id_part, axis=1).astype(jnp.float32)
        coupling = jnp.einsum("ltm,tim->lti", picked, phi_part.astype(jnp.float32))
        response = diag_part[None, :, :] * load_part.astype(jnp.float32) + coupling
        response = jnp.where(live_slot[None, :, None], response, jnp.zeros_like(response))
        row_totals = jnp.sum(response * state_part.astype(jnp.float32), axis=2) * sens_scale
        member = (owner_sub[:, None] == jnp.arange(SUBS_DEV, dtype=jnp.int32)[None, :]) & live_slot[:, None]
        sensitivity = jnp.dot(row_totals, member.astype(jnp.float32), precision=lax.Precision.HIGHEST)
        return response.astype(jnp.bfloat16), sensitivity

    adjoint_parts, sens_parts = lax.map(recover, (load_tiles, state_tiles, diag_tiles, phi_tiles, block_ids, group_sizes))
    adjoint = adjoint_parts.transpose(1, 0, 2, 3).reshape(LOADS, ROWS)
    sensitivity = sens_parts.transpose(1, 0, 2).reshape(LOADS, SUBS)
    return (adjoint, sensitivity)
```

```python
import functools
import itertools
import jax
import jax.numpy as jnp
from jax import lax
from jax.experimental import pallas as pl
from jax.experimental.pallas import tpu as pltpu
from jax.sharding import PartitionSpec as P

sens_scale = 0.0625
MESH = pl.DeviceIdType.MESH
VMEM_LIMIT = 60 * 1024 * 1024
STEP_TILES = 64


def condense_kernel(tiles, inc_ref, live_ref, loads_ref, phi_ref, out_ref, acc_ref):
    step = pl.program_id(0)
    width = phi_ref.shape[1]

    @pl.when(step == 0)
    def _():
        acc_ref[...] = jnp.zeros_like(acc_ref)

    for j in range(tiles):
        t = step * tiles + j
        term = jnp.dot(
            loads_ref[:, j * width : (j + 1) * width],
            phi_ref[j],
            preferred_element_type=jnp.float32,
        )
        term = jnp.where(t < live_ref[0], term, jnp.zeros_like(term))
        b = inc_ref[t]
        acc_ref[b] = acc_ref[b] + term

    @pl.when(step == pl.num_programs(0) - 1)
    def _():
        chunks, _, rows, _ = out_ref.shape
        for c in range(chunks):
            out_ref[c] = acc_ref[:, c * rows : (c + 1) * rows, :].astype(out_ref.dtype)


def recover_kernel(
    tiles, inc_ref, live_ref, loads_ref, state_ref, diag_ref, phi_ref, amp_ref, first_ref, last_ref,
    adj_ref, sens_ref, acc_ref,
):
    step = pl.program_id(0)
    width = phi_ref.shape[1]

    @pl.when(step == 0)
    def _():
        acc_ref[...] = jnp.zeros_like(acc_ref)

    total = acc_ref[...]
    for j in range(tiles):
        t = step * tiles + j
        cols = slice(j * width, (j + 1) * width)
        b = inc_ref[t]
        amp = jnp.concatenate([amp_ref[c, b] for c in range(amp_ref.shape[0])], axis=0)
        coupling = lax.dot_general(
            amp, phi_ref[j], (((1,), (1,)), ((), ())),
            preferred_element_type=jnp.float32,
        )
        response = diag_ref[:, cols] * loads_ref[:, cols].astype(jnp.float32) + coupling
        response = jnp.where(t < live_ref[0], response, jnp.zeros_like(response))
        adj_ref[:, cols] = response.astype(adj_ref.dtype)
        row_total = jnp.sum(response * state_ref[:, cols].astype(jnp.float32), axis=1, keepdims=True)
        member = ((first_ref[...] <= t) & (t < last_ref[...])).astype(jnp.float32)
        total = total + row_total * member
    acc_ref[...] = total

    @pl.when(step == pl.num_programs(0) - 1)
    def _():
        sens_ref[...] = acc_ref[...] * sens_scale


ORDER = "01C01C01CC001000110110101011"


def chunks_of(load_rows):
    return 2 if load_rows % 32 == 0 else 1


def exchange_kernel(wide, narrow, names, part_ref, factor_ref, out_ref, *scratch):
    ref = dict(zip(names, scratch))
    fac, stage, stage_sem = ref["fac"], ref["stage"], ref["stage_sem"]
    own_w, own_n = lax.axis_index("wide"), lax.axis_index("narrow")
    half = wide // 2
    pair, core = own_w // 2, own_w % 2
    partner = own_w + 1 - 2 * core
    chunks, _, own_blocks, rows, width = part_ref.shape
    total_rows = rows * narrow
    own_rows, own_cols = fac.shape
    cols = own_cols // wide
    pieces = 2
    blocks = own_blocks // pieces
    lines = total_rows // pieces
    bf = part_ref.dtype
    f32 = jnp.float32

    def flipped(index, by, count):
        for k in range(count.bit_length() - 1):
            b = 1 << k
            index = index + ((by // b) % 2) * b * (1 - 2 * ((index // b) % 2))
        return index

    def same(r):
        return 2 * flipped(pair, r, half) + core

    def cross(r):
        return 2 * flipped(pair, r, half) + 1 - core

    peers = [flipped(own_n, i, narrow) for i in range(narrow)]
    far = list(range(half - 1, 0, -1))
    near = list(range(1, half))
    away = list(range(narrow - 1, 0, -1))

    slots, stage_rows, _ = stage.shape
    stages = own_rows // stage_rows

    def load(s):
        return pltpu.make_async_copy(
            factor_ref.at[pl.ds(s * stage_rows, stage_rows)], stage.at[s % slots], stage_sem.at[s % slots]
        )

    for s in range(min(slots, stages)):
        load(s).start()

    barrier = pltpu.get_barrier_semaphore()
    greeted = [(partner, own_n)] + [(cross(r), own_n) for r in far] + [(own_w, peers[i]) for i in away]
    for device in greeted:
        pl.semaphore_signal(barrier, inc=1, device_id=device, device_id_type=MESH)
    pl.semaphore_wait(barrier, len(greeted))

    sends = []

    def send(src, dst, ssem, rsem, device, keep=True):
        pltpu.make_async_remote_copy(
            src_ref=src, dst_ref=dst, send_sem=ssem, recv_sem=rsem, device_id=device, device_id_type=MESH
        ).start()
        if keep:
            sends.append((src, ssem))

    def sent(src, ssem):
        pltpu.make_async_remote_copy(
            src_ref=src, dst_ref=src, send_sem=ssem, recv_sem=ssem, device_id=(partner, own_n), device_id_type=MESH
        ).wait_send()

    def arrived(dst, rsem):
        pltpu.make_async_remote_copy(
            src_ref=dst, dst_ref=dst, send_sem=rsem, recv_sem=rsem, device_id=(partner, own_n), device_id_type=MESH
        ).wait_recv()

    def spread(buf, cut, sems, p):
        own = buf.at[own_w].at[cut(p)]
        xs, xr, ps, pr = sems
        for r in far:
            send(own, own, xs.at[r, p], xr.at[r, p], (cross(r), own_n))
        send(own, own, ps.at[0, p], pr.at[0, p], (partner, own_n))

    def relay(buf, cut, sems, p, r):
        xs, xr, ps, pr = sems
        got = buf.at[cross(r)].at[cut(p)]
        arrived(got, xr.at[r, p])
        send(got, got, ps.at[r, p], pr.at[r, p], (partner, own_n))

    def relayed(buf, cut, sems, p, r):
        slot = same(r) if r else partner
        arrived(buf.at[slot].at[cut(p)], sems[3].at[r, p])

    def block_cut(p):
        return pl.ds(p * blocks, blocks)

    def line_cut(p):
        return pl.ds(p * lines, lines)

    def convert():
        for s in range(stages):
            load(s).wait()
            step = stage_rows // 8

            def some(r, carry, s=s):
                here = pl.multiple_of(r * step, step)
                fac[pl.ds(s * stage_rows + here, step), :] = stage[s % slots, pl.ds(here, step), :].astype(bf)
                return carry

            lax.fori_loop(0, 8, some, 0)
            if s + slots < stages:
                load(s + slots).start()
            if (s + 1) % max(1, stages // 4) == 0:
                yield

    def run(c):
        part = part_ref.at[c]
        c1, c2, cs, held = (ref[k].at[c] for k in ("c1", "c2", "cs", "held"))
        c1s, c1r, c2s, c2r = (ref[k].at[c] for k in ("c1_s", "c1_r", "c2_s", "c2_r"))
        hs, hr = ref["held_s"].at[c], ref["held_r"].at[c]
        for p in range(pieces):
            for r in far:
                send(part.at[same(r), block_cut(p)], c1.at[r, block_cut(p)], c1s.at[r, p], c1r.at[r, p], (partner, own_n))
        for p in range(pieces):
            send(part.at[partner, block_cut(p)], c1.at[0, block_cut(p)], c1s.at[0, p], c1r.at[0, p], (partner, own_n))
        yield
        for p in range(pieces):
            for r in far:
                at = block_cut(p)
                arrived(c1.at[r, at], c1r.at[r, p])
                cs[r - 1, at] = (part[cross(r), at].astype(f32) + c1[r, at].astype(f32)).astype(bf)
                send(cs.at[r - 1, at], c2.at[r - 1, at], c2s.at[r, p], c2r.at[r, p], (cross(r), own_n))
        yield
        for p in range(pieces):
            at = block_cut(p)
            arrived(c1.at[0, at], c1r.at[0, p])
            total = part[own_w, at].astype(f32) + c1[0, at].astype(f32)
            for r in near:
                arrived(c2.at[r - 1, at], c2r.at[r, p])
                total = total + c2[r - 1, at].astype(f32)
            held[0, at] = total.astype(bf)
            for i in away:
                send(held.at[0, at], held.at[i, at], hs.at[i, p], hr.at[i, p], (own_w, peers[i]))
        yield
        lhs = ref["lhs"].at[c]
        for i in range(narrow):
            for p in range(pieces):
                if i:
                    arrived(held.at[i, block_cut(p)], hr.at[i, p])
            for b in range(own_blocks):
                lhs[i * rows : (i + 1) * rows, b * width : (b + 1) * width] = held[i, b]
        i1, i2, isb, given, own_sum, image = (ref[k].at[c] for k in ("i1", "i2", "is", "given", "own_sum", "image"))
        i1s, i1r, i2s, i2r = (ref[k].at[c] for k in ("i1_s", "i1_r", "i2_s", "i2_r"))

        def product(slot):
            here = pl.multiple_of(slot * cols, cols)
            return jnp.dot(lhs[...], fac[:, pl.ds(here, cols)], preferred_element_type=f32)

        def give(j, carry):
            r = half - 1 - j
            other = (r + half - 1) // half
            slot = 2 * flipped(pair, r, half) + core * other + (1 - core) * (1 - other)
            given[r] = product(slot).astype(bf)
            for p in range(pieces):
                at = line_cut(p)
                send(given.at[r, at], i1.at[r, at], i1s.at[r, p], i1r.at[r, p], (partner, own_n), keep=False)
            return carry

        lax.fori_loop(0, half, give, 0)

        def keep(j, carry):
            r = half - 1 - j
            value = product(cross(r))
            for p in range(pieces):
                arrived(i1.at[r, line_cut(p)], i1r.at[r, p])
            isb[r - 1] = (value + i1[r].astype(f32)).astype(bf)
            for p in range(pieces):
                at = line_cut(p)
                send(isb.at[r - 1, at], i2.at[r - 1, at], i2s.at[r, p], i2r.at[r, p], (cross(r), own_n), keep=False)
            return carry

        lax.fori_loop(0, half - 1, keep, 0)
        for p in range(pieces):
            at = line_cut(p)
            sends.extend((given.at[r, at], i1s.at[r, p]) for r in range(half))
            sends.extend((isb.at[r - 1, at], i2s.at[r, p]) for r in near)
        own_sum[...] = product(own_w)
        yield
        im = tuple(ref["im" + k].at[c] for k in ("_xs", "_xr", "_ps", "_pr"))
        for p in range(pieces):
            at = line_cut(p)
            arrived(i1.at[0, at], i1r.at[0, p])
            total = own_sum[at] + i1[0, at].astype(f32)
            for r in near:
                arrived(i2.at[r - 1, at], i2r.at[r, p])
                total = total + i2[r - 1, at].astype(f32)
            image[own_w, at] = total.astype(bf)
            spread(image, line_cut, im, p)
        yield
        acc, amp, amp_in = ref["acc"].at[c], ref["amp"].at[c], ref["amp_in"].at[c]
        as_, ar = ref["amp_s"].at[c], ref["amp_r"].at[c]
        tile = min(4 * width, own_rows // pieces)
        tiles = own_rows // tile

        def contract(q, first, last, t):
            here = pl.multiple_of(t * tile, tile)
            there = pl.multiple_of(2 * q * cols, 2 * cols)
            left = jnp.concatenate([image[2 * q], image[2 * q + 1]], axis=1)
            value = lax.dot_general(
                left, fac[pl.ds(here, tile), pl.ds(there, 2 * cols)], (((1,), (1,)), ((), ())),
                preferred_element_type=f32,
            )
            if not first:
                value = value + acc[:, pl.ds(here, tile)]
            if not last:
                acc[:, pl.ds(here, tile)] = value
                return
            value = value.astype(bf)
            for i in range(narrow):
                for h in range(tile // width):
                    amp[i, t * (tile // width) + h] = value[i * rows : (i + 1) * rows, h * width : (h + 1) * width]

        def contract_some(q, first, last, lo, hi):
            def one(t, carry):
                contract(q, first, last, t)
                return carry

            lax.fori_loop(lo, hi, one, 0)

        for p in range(pieces):
            relayed(image, line_cut, im, p, 0)
        contract_some(pair, True, half == 1, 0, tiles)
        yield
        for p in range(pieces):
            for r in near:
                relay(image, line_cut, im, p, r)
        yield
        for r in near[:-1]:
            for p in range(pieces):
                relayed(image, line_cut, im, p, r)
            contract_some(flipped(pair, r, half), False, False, 0, tiles)
        for r in near[-1:]:
            for p in range(pieces):
                relayed(image, line_cut, im, p, r)
            for p in range(pieces):
                contract_some(flipped(pair, r, half), False, True, tiles * p // pieces, tiles * (p + 1) // pieces)
                at = block_cut(p)
                for i in away:
                    send(amp.at[i, at], amp_in.at[i - 1, at], as_.at[i, p], ar.at[i, p], (own_w, peers[i]))
        yield
        out = out_ref.at[c]
        om = tuple(ref["out" + k].at[c] for k in ("_xs", "_xr", "_ps", "_pr"))
        for p in range(pieces):
            at = block_cut(p)
            total = amp[0, at].astype(f32)
            for i in away[::-1]:
                arrived(amp_in.at[i - 1, at], ar.at[i, p])
                total = total + amp_in[i - 1, at].astype(f32)
            out[own_w, at] = total.astype(bf)
            spread(out, block_cut, om, p)
        yield
        for p in range(pieces):
            for r in near:
                relay(out, block_cut, om, p, r)
        yield
        for p in range(pieces):
            for r in [0] + near:
                relayed(out, block_cut, om, p, r)

    runs = {str(c): run(c) for c in range(chunks)}
    runs["C"] = convert()
    for who in ORDER:
        if who in runs:
            next(runs[who], None)
    for gen in runs.values():
        for _ in gen:
            pass
    for src, ssem in sends:
        sent(src, ssem)


def exchange(partial, factor, wide, narrow):
    chunks, _, own_blocks, rows, width = partial.shape
    own_rows, own_cols = factor.shape
    cols = own_cols // wide
    half = wide // 2
    total_rows = rows * narrow
    bf, f32 = partial.dtype, jnp.float32
    dma = pltpu.SemaphoreType.DMA
    pieces = 2
    stage_rows = min(128, own_rows)
    slot = (own_blocks, rows, width)
    strip = (total_rows, cols)
    spec = {
        "fac": pltpu.VMEM((own_rows, own_cols), bf),
        "stage": pltpu.VMEM((4, stage_rows, own_cols), factor.dtype),
        "stage_sem": dma((4,)),
        "c1": pltpu.VMEM((chunks, half) + slot, bf),
        "c2": pltpu.VMEM((chunks, half - 1) + slot, bf),
        "cs": pltpu.VMEM((chunks, half - 1) + slot, bf),
        "held": pltpu.VMEM((chunks, narrow) + slot, bf),
        "lhs": pltpu.VMEM((chunks, total_rows, own_rows), bf),
        "i1": pltpu.VMEM((chunks, half) + strip, bf),
        "i2": pltpu.VMEM((chunks, half - 1) + strip, bf),
        "is": pltpu.VMEM((chunks, half - 1) + strip, bf),
        "given": pltpu.VMEM((chunks, half) + strip, bf),
        "own_sum": pltpu.VMEM((chunks,) + strip, f32),
        "image": pltpu.VMEM((chunks, wide) + strip, bf),
        "acc": pltpu.VMEM((chunks, total_rows, own_rows), f32),
        "amp": pltpu.VMEM((chunks, narrow) + slot, bf),
        "amp_in": pltpu.VMEM((chunks, narrow - 1) + slot, bf),
    }
    for k in ("c1_s", "c1_r", "c2_s", "c2_r", "i1_s", "i1_r", "i2_s", "i2_r"):
        spec[k] = dma((chunks, half, pieces))
    for k in ("held_s", "held_r", "amp_s", "amp_r"):
        spec[k] = dma((chunks, narrow, pieces))
    for a in ("im", "out"):
        for k in ("_xs", "_xr", "_ps", "_pr"):
            spec[a + k] = dma((chunks, half, pieces))
    return pl.pallas_call(
        functools.partial(exchange_kernel, wide, narrow, tuple(spec)),
        out_shape=jax.ShapeDtypeStruct(partial.shape, bf),
        in_specs=[pl.BlockSpec(memory_space=pltpu.VMEM), pl.BlockSpec(memory_space=pl.ANY)],
        out_specs=pl.BlockSpec(memory_space=pltpu.VMEM),
        scratch_shapes=list(spec.values()),
        compiler_params=pltpu.CompilerParams(
            collective_id=0, has_side_effects=True, vmem_limit_bytes=VMEM_LIMIT
        ),
        name="exchange",
    )(partial, factor)


def body(loads, state, modal_diag, phi, incidence, sizes, factor):
    load_cols = loads.shape[0]
    tile_count, width, _ = phi.shape
    subs_local = sizes.shape[0]
    wide, narrow = lax.axis_size("wide"), lax.axis_size("narrow")
    own_blocks = factor.shape[0] // width
    block_count = own_blocks * wide
    running = jnp.cumsum(sizes)
    live = running[-1:]
    tiles = min(STEP_TILES, tile_count)
    steps = tile_count // tiles
    params = pltpu.CompilerParams(dimension_semantics=("arbitrary",), vmem_limit_bytes=VMEM_LIMIT)
    row_spec = pl.BlockSpec((load_cols, tiles * width), lambda s, *_: (0, s))
    phi_spec = pl.BlockSpec((tiles, width, width), lambda s, *_: (s, 0, 0))
    chunks = chunks_of(load_cols)
    chunk_shape = (chunks, block_count, load_cols // chunks, width)
    amp_spec = pl.BlockSpec(chunk_shape, lambda s, *_: (0, 0, 0, 0))
    sub_spec = pl.BlockSpec((1, subs_local), lambda s, *_: (0, 0))
    sens_spec = pl.BlockSpec((load_cols, subs_local), lambda s, *_: (0, 0))

    partial = pl.pallas_call(
        functools.partial(condense_kernel, tiles),
        out_shape=jax.ShapeDtypeStruct(chunk_shape, jnp.bfloat16),
        grid_spec=pltpu.PrefetchScalarGridSpec(
            num_scalar_prefetch=2, grid=(steps,), in_specs=[row_spec, phi_spec], out_specs=amp_spec,
            scratch_shapes=[pltpu.VMEM((block_count, load_cols, width), jnp.float32)],
        ),
        compiler_params=params,
        name="condense",
    )(incidence, live, loads, phi)
    amp = exchange(
        partial.reshape(chunks, wide, own_blocks, load_cols // chunks, width), factor, wide, narrow
    ).reshape(chunk_shape)
    adjoint, sensitivity = pl.pallas_call(
        functools.partial(recover_kernel, tiles),
        out_shape=(
            jax.ShapeDtypeStruct(loads.shape, jnp.bfloat16),
            jax.ShapeDtypeStruct((load_cols, subs_local), jnp.float32),
        ),
        grid_spec=pltpu.PrefetchScalarGridSpec(
            num_scalar_prefetch=2, grid=(steps,),
            in_specs=[
                row_spec, row_spec, pl.BlockSpec((1, tiles * width), lambda s, *_: (0, s)),
                phi_spec, amp_spec, sub_spec, sub_spec,
            ],
            out_specs=(row_spec, sens_spec),
            scratch_shapes=[pltpu.VMEM((load_cols, subs_local), jnp.float32)],
        ),
        compiler_params=params,
        name="recover",
    )(
        incidence, live, loads, state, modal_diag.reshape(1, -1), phi, amp,
        (running - sizes).reshape(1, -1), running.reshape(1, -1),
    )
    return (adjoint, sensitivity)


def solution(mesh):
    return jax.shard_map(
        body,
        mesh=mesh,
        in_specs=(
            P("narrow", "wide"),
            P("narrow", "wide"),
            P("wide"),
            P("wide", None, None),
            P("wide"),
            P("wide"),
            P("wide", "narrow"),
        ),
        out_specs=(P("narrow", "wide"), P("narrow", "wide")),
        check_vma=False,
    )
```
